32 devices in a mesh: seq: 4 (over z), batch: 8 (over y, x, core).
Axes of the slice: x: 2, y: 2, z: 4, core: 2. Of those that a mesh axis runs over, the one named last changes fastest.
Arguments:
- queries: bfloat16 [8, 2048, 2048], P('batch', 'seq'), may hold values from -6 to 6
- keys: bfloat16 [8, 2048, 2048], P('batch', 'seq'), may hold values from -6 to 6
- values: bfloat16 [8, 2048, 2048], P('batch', 'seq'), may hold values from -6 to 6
- level_gain: float32 [8, 2048, 128], P('batch', 'seq'), may hold values from 0.004 to 0.06
- out_weight: bfloat16 [2048, 2048], P('batch'), may hold values from -0.125 to 0.125
- out_grad: bfloat16 [8, 2048, 2048], P('batch', 'seq'), may hold values from -6 to 6
Outputs:
- query_grad: bfloat16 [8, 2048, 2048], P('batch', 'seq')
- key_grad: bfloat16 [8, 2048, 2048], P('batch', 'seq')
- value_grad: bfloat16 [8, 2048, 2048], P('batch', 'seq')
- gain_grad: float32 [8, 2048, 128], P('batch', 'seq')
- weight_grad: float32 [2048, 2048], P(('seq', 'batch'))
The draws below stay inside these ranges and needn't reach their ends.
All inputs are finite; a program needn't handle non-finite values.
Results may differ from the reference program's by a relative error of at most 0.0064.
Values may be sent and summed in bfloat16 or wider, within the bound.
No kernel may reach another device: no remote copies, remote signals or barrier semaphores. Data moves between devices by JAX's collectives and lax.ppermute only.
A program may use at most 192 MiB of HBM per device.

```python
import math
import jax
import jax.numpy as jnp
import numpy as np
from jax import lax

H = 16
HD = 128
D = 2048
TOK_DEV = 512
GROUP = 64
LEVELS = 8
TOKENS = 2048
BATCH = 8
N_SEQ = 4


def shard_levels(own_key, shape, shards, least, top_value):
    factor_of, own = 1.0, jax.random.fold_in(own_key, 6)
    for axis_at, shards_of in shards:
        heights = jnp.exp(jax.random.uniform(jax.random.fold_in(own, axis_at), (shards_of,), jnp.float32, least / len(shards), top_value / len(shards)))
        factor_of = factor_of * jnp.repeat(heights, shape[axis_at] // shards_of).reshape([-1 if axis == axis_at else 1 for axis in range(len(shape))])
    return factor_of


def normal_values(key, dims, spread, limit, shards=(), held_as=jnp.bfloat16):
    loudness = shard_levels(key, dims, shards, -0.22, 0.18) if shards else 1.0
    values = jax.random.normal(key, dims, jnp.float32) * spread * loudness
    return jnp.minimum(jnp.maximum(values, -limit), limit).astype(held_as)


def setup_inputs(seed: int = 0) -> dict:
    seeds = jax.random.split(jax.random.key(seed), 7)
    return {
        "queries": normal_values(seeds[0], (BATCH, TOKENS, D), 1.0, 6.0, ((0, 8), (1, 4))),
        "keys": normal_values(seeds[1], (BATCH, TOKENS, D), 1.0, 6.0, ((0, 8), (1, 4))),
        "values": normal_values(seeds[2], (BATCH, TOKENS, D), 1.0, 6.0, ((0, 8), (1, 4))),
        "level_gain": jnp.clip(jnp.exp(math.log(0.06) - 2.70805 * jax.random.uniform(seeds[3], (BATCH, TOKENS, LEVELS * H), jnp.float32) ** shard_levels(seeds[3], (BATCH, TOKENS, LEVELS * H), ((0, 8), (1, 4)), -0.2, 0.2)), 0.004, 0.06),
        "out_weight": normal_values(seeds[4], (D, D), D ** -0.5, 0.125, ((0, 8),)),
        "out_grad": normal_values(seeds[5], (BATCH, TOKENS, D), 1.0, 6.0, ((0, 8), (1, 4))),
    }


def level_selects(seg_len):
    loc_bits = (seg_len // GROUP).bit_length() - 1
    position = np.arange(seg_len, dtype=np.int32)
    group_id = position // GROUP
    crossed = group_id[:, None] ^ group_id[None, :]
    level_id = np.zeros((seg_len, seg_len), np.int32)
    for shift_bit in range(loc_bits):
        level_id = level_id + ((crossed >> shift_bit) > 0).astype(np.int32)
    causal = position[None, :] <= position[:, None]
    return [jnp.asarray(((level_id == level_num) & causal).astype(np.float32), jnp.float32) for level_num in range(loc_bits + 1)]


def segment_tables(n_bits):
    seg_ids = np.arange(N_SEQ)
    target = seg_ids[:, None]
    source = seg_ids[None, :]
    tables = []
    for level_bit in range(n_bits):
        member = (((target >> level_bit) & 1) == 1) & (((source >> level_bit) & 1) == 0) & ((target >> (level_bit + 1)) == (source >> (level_bit + 1)))
        tables.append(member.astype(np.float32))
    return jnp.asarray(np.stack(tables), jnp.float32)


def to_bf16(array):
    return lax.optimization_barrier(array.astype(jnp.bfloat16)).astype(jnp.float32)


def segment_pass(seg_query, seg_key, seg_value, seg_gain, seg_dout, far_stack, selects):
    seg_len = seg_query.shape[0]
    loc_bits = len(selects) - 1
    n_bits = far_stack.shape[0]
    score_scale = HD ** -0.5
    highest = lax.Precision.HIGHEST
    query_wide = seg_query.reshape(seg_len, H, HD).astype(jnp.float32)
    key_wide = seg_key.reshape(seg_len, H, HD).astype(jnp.float32)
    value_wide = seg_value.reshape(seg_len, H, HD).astype(jnp.float32)
    grad_wide = seg_dout.reshape(seg_len, H, HD).astype(jnp.float32)
    gains = seg_gain.reshape(seg_len, LEVELS, H)
    far_half = to_bf16(far_stack)
    scores = jnp.einsum('thd,shd->hts', query_wide, key_wide, precision=highest) * score_scale
    weight_mask = jnp.zeros((H, seg_len, seg_len), jnp.float32)
    for level_num in range(loc_bits + 1):
        weight_mask = weight_mask + selects[level_num][None] * gains[:, level_num, :].T[:, :, None]
    probs = to_bf16(scores * weight_mask)
    intra = jnp.einsum('hts,shd->thd', probs, value_wide, precision=highest)
    far_gain = jnp.transpose(gains[:, loc_bits + 1:loc_bits + 1 + n_bits, :], (1, 0, 2))
    projected = jnp.einsum('thd,bhde->bthe', query_wide, far_half, precision=highest) * score_scale
    cross = jnp.sum(far_gain[..., None] * projected, axis=0)
    attn = (intra + cross).reshape(seg_len, H * HD).astype(jnp.bfloat16)
    prob_grad = jnp.einsum('thd,shd->hts', grad_wide, value_wide, precision=highest)
    grad_v_in = jnp.einsum('hts,thd->shd', probs, grad_wide, precision=highest)
    energy = prob_grad * scores
    local_gain = jnp.stack([jnp.sum(energy * sel_mat[None], axis=2).T for sel_mat in selects], axis=1)
    score_grad = to_bf16(prob_grad * weight_mask)
    grad_q_in = jnp.einsum('hts,shd->thd', score_grad, key_wide, precision=highest) * score_scale
    grad_k_in = jnp.einsum('hts,thd->shd', score_grad, query_wide, precision=highest) * score_scale
    weighted = to_bf16(far_gain[..., None] * grad_wide[None])
    grad_q_far = jnp.einsum('bthe,bhde->thd', weighted, far_half, precision=highest) * score_scale
    cross_gain = jnp.transpose(jnp.sum(projected * grad_wide[None], axis=3), (1, 0, 2))
    weighted_query = to_bf16(far_gain[..., None] * query_wide[None])
    far_grad = jnp.einsum('bthd,the->bhde', weighted_query, grad_wide, precision=highest) * score_scale
    spare = LEVELS - loc_bits - 1 - n_bits
    gain_grad = jnp.concatenate([local_gain, cross_gain, jnp.zeros((seg_len, spare, H), jnp.float32)], axis=1)
    return attn, grad_q_in + grad_q_far, grad_k_in, grad_v_in, gain_grad.reshape(seg_len, LEVELS * H), far_grad


def reference(queries, keys, values, level_gain, out_weight, out_grad):
    highest = lax.Precision.HIGHEST
    n_bits = N_SEQ.bit_length() - 1
    selects = level_selects(TOK_DEV)
    tables = segment_tables(n_bits)
    attn_grad = jnp.dot(out_grad.reshape(BATCH * TOKENS, D), out_weight.T, preferred_element_type=jnp.float32).astype(jnp.bfloat16).reshape(BATCH, TOKENS, D)

    def batch_pass(items):
        seq_query, seq_key, seq_value, seq_gain, seq_dout = items
        seg_query = seq_query.reshape(N_SEQ, TOK_DEV, D)
        seg_key = seq_key.reshape(N_SEQ, TOK_DEV, D)
        seg_value = seq_value.reshape(N_SEQ, TOK_DEV, D)
        seg_gain = seq_gain.reshape(N_SEQ, TOK_DEV, LEVELS * H)
        seg_dout = seq_dout.reshape(N_SEQ, TOK_DEV, D)
        key_heads = seg_key.reshape(N_SEQ, TOK_DEV, H, HD).astype(jnp.float32)
        value_heads = seg_value.reshape(N_SEQ, TOK_DEV, H, HD).astype(jnp.float32)
        states = jnp.einsum('nthd,nthe->nhde', key_heads, value_heads, precision=highest)
        far_all = jnp.einsum('bnm,mhde->nbhde', tables, states, precision=highest)

        def one_segment(seg_items):
            return segment_pass(*seg_items, selects)

        attn, grad_q, grad_k_in, grad_v_in, gain_grad, far_grad = lax.map(one_segment, (seg_query, seg_key, seg_value, seg_gain, seg_dout, far_all))
        state_grad = jnp.einsum('bnm,nbhde->mhde', tables, far_grad, precision=highest)
        state_half = to_bf16(state_grad)
        grad_k = grad_k_in + jnp.einsum('nshe,nhde->nshd', value_heads, state_half, precision=highest)
        grad_v = grad_v_in + jnp.einsum('nshd,nhde->nshe', key_heads, state_half, precision=highest)
        return (attn.reshape(TOKENS, D), grad_q.reshape(TOKENS, D).astype(jnp.bfloat16), grad_k.reshape(TOKENS, D).astype(jnp.bfloat16), grad_v.reshape(TOKENS, D).astype(jnp.bfloat16), gain_grad.reshape(TOKENS, LEVELS * H))

    attn, query_grad, key_grad, value_grad, gain_grad = lax.map(batch_pass, (queries, keys, values, level_gain, attn_grad))
    weight_grad = lax.dot_general(attn.reshape(BATCH * TOKENS, D), out_grad.reshape(BATCH * TOKENS, D), (((0,), (0,)), ((), ())), preferred_element_type=jnp.float32)
    return query_grad, key_grad, value_grad, gain_grad, weight_grad
```

```python
import functools

import jax
import jax.numpy as jnp
from jax import lax
from jax.experimental import pallas as pl
from jax.experimental.pallas import tpu as pltpu
from jax.sharding import PartitionSpec as P

H = 16
HD = 128
GROUP = 64
LEVELS = 8
HALF = 2 * GROUP
TILE = 4 * GROUP
SCALE = HD ** (-0.5)
BF = jnp.bfloat16
F32 = jnp.float32


def swapped(value, axis, mask):
    return lax.ppermute(value, axis, [(source, source ^ mask) for source in range(lax.axis_size(axis))])


def mm(a, b, ca, cb):
    return lax.dot_general(a, b, (((ca,), (cb,)), ((), ())), preferred_element_type=F32)


def call(body, flops, nbytes, vmem=60, **kwargs):
    return pl.pallas_call(
        body,
        cost_estimate=pl.CostEstimate(flops=int(flops), bytes_accessed=int(nbytes), transcendentals=0),
        compiler_params=pltpu.CompilerParams(vmem_limit_bytes=vmem * 1024 * 1024),
        **kwargs,
    )


def level_columns(gain_ref, head, levels):
    rolled = pltpu.roll(gain_ref[...], lax.rem(LEVELS * H - head, LEVELS * H), 1)
    return {level: rolled[:, level * H : level * H + 1] for level in levels}


def half_masks():
    row = lax.broadcasted_iota(jnp.int32, (HALF, HALF), 0)
    col = lax.broadcasted_iota(jnp.int32, (HALF, HALF), 1)
    same = (row >= GROUP) == (col >= GROUP)
    return same & (col <= row), (row >= GROUP) & (col < GROUP)


def tile_weight(w, start, own, below):
    first, second = slice(start, start + HALF), slice(start + HALF, start + TILE)
    zero = jnp.zeros((HALF, HALF), F32)

    def corner(rows):
        return jnp.where(own, w[0][rows], jnp.where(below, w[1][rows], 0.0))

    side = jnp.broadcast_to(w[2][second], (HALF, HALF))
    top = jnp.concatenate([corner(first), zero], axis=1)
    bottom = jnp.concatenate([side, corner(second)], axis=1)
    return jnp.concatenate([top, bottom], axis=0)


def far_blocks(seg_len):
    blocks = []
    size, level = TILE, 3
    while size < seg_len:
        for start in range(0, seg_len, 2 * size):
            blocks.append((level, start + size, start, size))
        size, level = 2 * size, level + 1
    return blocks


def states_body(k_ref, v_ref, wide_ref, half_ref, block_ref):
    seg_len = k_ref.shape[0]
    for i in range(wide_ref.shape[0]):
        cols = slice(i * HD, (i + 1) * HD)
        tiles = [
            mm(k_ref[start : start + TILE, cols], v_ref[start : start + TILE, cols], 0, 0)
            for start in range(0, seg_len, TILE)
        ]
        state = sum(tiles[1:], tiles[0])
        wide_ref[i] = state
        half_ref[i] = state.astype(BF)
        for j, (_, _, col, size) in enumerate(far_blocks(seg_len)):
            part = tiles[col // TILE : (col + size) // TILE]
            block_ref[j, i] = sum(part[1:], part[0]).astype(BF)


def intra_body(n_bits, heads, bits_ref, q_ref, k_ref, v_ref, gain_ref, block_ref, out_ref, wq_ref):
    seg_len = q_ref.shape[0]
    loc_bits = (seg_len // GROUP).bit_length() - 1
    own, below = half_masks()
    for i in range(heads):
        cols = slice(i * HD, (i + 1) * HD)
        w = level_columns(gain_ref, pl.program_id(0) * heads + i, range(loc_bits + 1 + n_bits))
        for b in range(n_bits):
            factor = w[loc_bits + 1 + b] * bits_ref[b].astype(F32)
            at = (i * n_bits + b) * HD
            wq_ref[:, at : at + HD] = (q_ref[:, cols].astype(F32) * factor).astype(BF)
        for start in range(0, seg_len, TILE):
            rows = slice(start, start + TILE)
            scores = mm(q_ref[rows, cols], k_ref[rows, cols], 1, 1) * SCALE
            probs = (scores * tile_weight(w, start, own, below)).astype(BF)
            total = mm(probs, v_ref[rows, cols], 1, 0)
            for j, (level, row, _, size) in enumerate(far_blocks(seg_len)):
                if row <= start < row + size:
                    total += mm(q_ref[rows, cols], block_ref[j, i], 1, 0) * (w[level][rows] * SCALE)
            out_ref[rows, cols] = total


def attn_body(n_bits, heads, at_ref, wq_ref, intra_ref, *refs):
    far_refs, out_ref = refs[:n_bits], refs[n_bits]
    for i in range(heads):
        cols = slice(i * HD, (i + 1) * HD)
        far = jnp.concatenate([ref[i] for ref in far_refs], axis=0)
        total = intra_ref[:, cols] + mm(wq_ref[:, i * n_bits * HD : (i + 1) * n_bits * HD], far, 1, 0) * SCALE
        place = pl.multiple_of((i ^ at_ref[1]) * HD, HD)
        out_ref[:, pl.ds(place, HD)] = total.astype(BF)


def weight_body(picks, core_ref, attn_ref, attn2_ref, gx_ref, gx2_ref, gy_ref, gy2_ref, outx_ref, outy_ref):
    del core_ref
    for pick, left, right, out_ref in (
        (picks[0], gx_ref, gx2_ref, outx_ref),
        (picks[1], gy_ref, gy2_ref, outy_ref),
    ):
        total = 0.0
        for ref, grad_ref in ((attn_ref, left), (attn2_ref, right)):
            lhs = jnp.concatenate([ref[:, p * HD : (p + 1) * HD] for p in pick], axis=1)
            total += mm(lhs, grad_ref[...], 0, 0)
        out_ref[...] = total.astype(out_ref.dtype)


def attn_grad_body(count, at_ref, dout_ref, *refs):
    del at_ref
    out_ref = refs[-1]
    for j in range(count):
        @pl.when(pl.program_id(0) == j)
        def _(j=j):
            out_ref[...] = mm(dout_ref[...], refs[j][...], 1, 1).astype(BF)


def far_grad_body(n_bits, heads, wq_ref, g_ref, half_ref, wide_ref):
    for i in range(heads):
        span = n_bits * HD
        grad = mm(wq_ref[:, i * span : (i + 1) * span], g_ref[:, i * HD : (i + 1) * HD], 0, 0) * SCALE
        for b in range(n_bits):
            part = grad[b * HD : (b + 1) * HD]
            half_ref[b, i] = part.astype(BF)
            wide_ref[b, i] = part


def far_grad_four_body(heads, at_ref, wq_ref, g_ref, half_ref, wide_ref):
    for i in range(heads):
        grad = mm(wq_ref[:, 2 * i * HD : 2 * (i + 1) * HD], g_ref[:, i * HD : (i + 1) * HD], 0, 0) * SCALE
        low, high = grad[:HD], grad[HD:]
        half_ref[i] = jnp.where(at_ref[0] == 2, high, low).astype(BF)
        wide_ref[i] = high


def main_body(n_bits, heads, offset, carried, bits_ref, q_ref, k_ref, v_ref, g_ref, gain_ref, block_ref, *refs):
    far_refs = refs[:n_bits]
    gq_ref, gk_ref, gv_ref, back_ref, gain_grad_ref, lev_ref = refs[n_bits + carried :]
    seg_len = q_ref.shape[0]
    loc_bits = (seg_len // GROUP).bit_length() - 1
    own, below = half_masks()
    lane = lax.broadcasted_iota(jnp.int32, (1, LEVELS * H), 1)

    @pl.when(pl.program_id(0) == 0)
    def _():
        if carried:
            gain_grad_ref[...] = refs[n_bits + carried - 1][...]
        else:
            gain_grad_ref[...] = jnp.zeros_like(gain_grad_ref)

    lev_ref[...] = jnp.zeros_like(lev_ref)

    def row_sum(x):
        return jnp.sum(x, axis=1, keepdims=True)

    for i in range(heads):
        head = offset + pl.program_id(0) * heads + i
        cols = slice(i * HD, (i + 1) * HD)
        w = level_columns(gain_ref, head, range(loc_bits + 1 + n_bits))
        far = jnp.concatenate([ref[i] for ref in far_refs], axis=0)

        def put(rows, column, level, head=head):
            pick = (lane == level * H + head).astype(F32)
            lev_ref[rows] += column * pick

        for start in range(0, seg_len, TILE):
            rows = slice(start, start + TILE)
            first, second = slice(start, start + HALF), slice(start + HALF, start + TILE)
            q, g = q_ref[rows, cols], g_ref[rows, cols]
            q_wide = q.astype(F32)
            back = mm(g, far, 1, 1)
            total = jnp.zeros((TILE, HD), F32)
            for b in range(n_bits):
                term = back[:, b * HD : (b + 1) * HD]
                bit = bits_ref[b].astype(F32)
                put(rows, row_sum(q_wide * term) * (SCALE * bit), loc_bits + 1 + b)
                total += term * (w[loc_bits + 1 + b][rows] * bit)
            for j, (level, row, _, size) in enumerate(far_blocks(seg_len)):
                if row <= start < row + size:
                    term = mm(g, block_ref[j, i], 1, 1)
                    put(rows, row_sum(q_wide * term) * SCALE, level)
                    total += term * w[level][rows]
            weight = tile_weight(w, start, own, below)
            scores = mm(q, k_ref[rows, cols], 1, 1) * SCALE
            prob_grad = mm(g, v_ref[rows, cols], 1, 1)
            energy = scores * prob_grad
            for half, at in ((first, 0), (second, HALF)):
                corner = energy[at : at + HALF, at : at + HALF]
                put(half, row_sum(jnp.where(own, corner, 0.0)), 0)
                put(half, row_sum(jnp.where(below, corner, 0.0)), 1)
            put(second, row_sum(energy[HALF:, :HALF]), 2)
            probs = (scores * weight).astype(BF)
            score_grad = (prob_grad * weight).astype(BF)
            total += mm(score_grad, k_ref[rows, cols], 1, 0)
            gq_ref[rows, cols] = (total * SCALE).astype(BF)
            gk_ref[rows, cols] = mm(score_grad, q, 0, 0) * SCALE
            gv_ref[rows, cols] = mm(probs, g, 0, 0)
        for j, (level, row, _, size) in enumerate(far_blocks(seg_len)):
            rows = slice(row, row + size)
            weighted = (q_ref[rows, cols].astype(F32) * w[level][rows]).astype(BF)
            back_ref[j, i] = mm(weighted, g_ref[rows, cols], 0, 0) * SCALE
    gain_grad_ref[...] += lev_ref[...]


def final_body(heads, shares_ref, k_ref, v_ref, gk_ref, gv_ref, back_ref, *refs):
    got_refs, (key_ref, value_ref) = refs[:-2], refs[-2:]
    seg_len = k_ref.shape[0]
    for i in range(heads):
        cols = slice(i * HD, (i + 1) * HD)
        state = jnp.zeros((HD, HD), F32)
        for b, ref in enumerate(got_refs):
            state += ref[i].astype(F32) * shares_ref[b].astype(F32)
        for start in range(0, seg_len, TILE):
            rows = slice(start, start + TILE)
            here = state
            for j, (_, _, col, size) in enumerate(far_blocks(seg_len)):
                if col <= start < col + size:
                    here = here + back_ref[j, i]
            half = here.astype(BF)
            key_ref[rows, cols] = (gk_ref[rows, cols] + mm(v_ref[rows, cols], half, 1, 1)).astype(BF)
            value_ref[rows, cols] = (gv_ref[rows, cols] + mm(k_ref[rows, cols], half, 1, 0)).astype(BF)


def sds(shape, dtype):
    return jax.ShapeDtypeStruct(shape, dtype)


def local(queries, keys, values, level_gain, out_weight, out_grad):
    outs = step(queries[0], keys[0], values[0], level_gain[0], out_weight, out_grad[0])
    return tuple(x[None] for x in outs[:4]) + (outs[4],)


def is_fast(seq_count, batch_count):
    return batch_count == 8 and seq_count * batch_count == 2 * H


def step(q, k, v, gain, out_weight, dout):
    seg_len, width = q.shape
    seq_count, batch_count = lax.axis_size("seq"), lax.axis_size("batch")
    n_bits = seq_count.bit_length() - 1
    seg_index, batch_index = lax.axis_index("seq"), lax.axis_index("batch")
    bits = jnp.stack([seg_index >> b & 1 for b in range(n_bits)]).astype(jnp.int32)
    fast = is_fast(seq_count, batch_count)
    prefetch = pltpu.PrefetchScalarGridSpec
    tok_bytes = seg_len * width * 2
    head_flops = 2 * seg_len * HD * HD * H
    n_blocks = len(far_blocks(seg_len))
    mats = (H, HD, HD)

    def cols(heads, scale=1):
        return pl.BlockSpec((seg_len, heads * HD * scale), lambda h, *_: (0, h))

    def mat(heads):
        return pl.BlockSpec((heads, HD, HD), lambda h, *_: (h, 0, 0))

    def stack(count, heads):
        return pl.BlockSpec((count, heads, HD, HD), lambda h, *_: (0, h, 0, 0))

    whole_gain = pl.BlockSpec((seg_len, LEVELS * H), lambda h, *_: (0, 0))

    state_wide, state_half, blocks = call(
        states_body, head_flops, 2 * tok_bytes,
        out_shape=(sds(mats, F32), sds(mats, BF), sds((n_blocks,) + mats, BF)),
        grid=(H // 4,), in_specs=[cols(4), cols(4)],
        out_specs=(mat(4), mat(4), stack(n_blocks, 4)),
    )(k, v)
    fars = []
    running_wide, running = state_wide, state_half
    for b in range(n_bits):
        received = swapped(running, "seq", 1 << b)
        fars.append(received)
        if b + 1 < n_bits:
            running_wide = running_wide + received.astype(F32)
            running = running_wide.astype(BF)

    if fast:
        pieces = {0: out_weight}
        rows = out_weight.shape[0]
        dout_pair = swapped(dout, "batch", 1)
        pieces[2] = swapped(out_weight, "batch", 2)
        pieces[4] = swapped(out_weight, "batch", 4)
        pieces[1] = swapped(out_weight, "batch", 1)
        diag_low = swapped(pieces[2][: rows // 2], "batch", 4)
        diag_high = swapped(pieces[4][rows // 2 :], "batch", 2)
        pieces[3] = swapped(pieces[2], "batch", 1)
        pieces[5] = swapped(pieces[4], "batch", 1)
        diag_low_pair = swapped(diag_low, "batch", 1)
        diag_high_pair = swapped(diag_high, "batch", 1)
        stages = [
            [(pieces[m], batch_index ^ m) for m in (0, 1)],
            [(pieces[m], batch_index ^ m) for m in (2, 3, 4, 5)],
            [
                (diag_low, (batch_index ^ 6) * 2),
                (diag_high, (batch_index ^ 6) * 2 + 1),
                (diag_low_pair, (batch_index ^ 7) * 2),
                (diag_high_pair, (batch_index ^ 7) * 2 + 1),
            ],
        ]
        g = None
        for stage in stages:
            count, piece_rows = len(stage), stage[0][0].shape[0]
            index = jnp.stack([at for _, at in stage]).astype(jnp.int32)
            arrays = [array for array, _ in stage]
            extra = [] if g is None else [g]
            g = call(
                functools.partial(attn_grad_body, count),
                2 * seg_len * width * piece_rows * count, tok_bytes + count * piece_rows * (width + seg_len) * 2,
                out_shape=sds((seg_len, width), BF),
                grid_spec=prefetch(
                    num_scalar_prefetch=1, grid=(count,),
                    in_specs=[pl.BlockSpec((seg_len, width), lambda j, at: (0, 0))]
                    + [pl.BlockSpec((piece_rows, width), lambda j, at: (0, 0))] * count
                    + [pl.BlockSpec(memory_space=pl.ANY)] * len(extra),
                    out_specs=pl.BlockSpec((seg_len, piece_rows), lambda j, at: (0, at[j])),
                ),
                input_output_aliases={} if g is None else {2 + count: 0},
            )(index, dout, *arrays, *extra)
    else:
        gathered = lax.all_gather(out_weight, "batch", axis=0, tiled=True)
        g = mm(dout, gathered, 1, 1).astype(BF)

    intra, wq = call(
        functools.partial(intra_body, n_bits, 4), 4 * seg_len * TILE * width, 7 * tok_bytes,
        out_shape=(sds((seg_len, width), F32), sds((seg_len, n_bits * width), BF)),
        grid_spec=prefetch(
            num_scalar_prefetch=1, grid=(H // 4,),
            in_specs=[cols(4), cols(4), cols(4), whole_gain, stack(n_blocks, 4)],
            out_specs=(cols(4), cols(4, n_bits)),
        ),
    )(bits, q, k, v, gain, blocks)

    at = jnp.stack([seg_index, batch_index >> 1]).astype(jnp.int32)
    if not fast:
        at = jnp.zeros_like(at)
    attn = call(
        functools.partial(attn_body, n_bits, 4), head_flops * n_bits, 5 * tok_bytes,
        out_shape=sds((seg_len, width), BF),
        grid_spec=prefetch(
            num_scalar_prefetch=1, grid=(H // 4,),
            in_specs=[
                pl.BlockSpec((seg_len, 4 * HD * n_bits), lambda j, a: (0, j ^ a[0])),
                pl.BlockSpec((seg_len, 4 * HD), lambda j, a: (0, j ^ a[0])),
            ]
            + [pl.BlockSpec((4, HD, HD), lambda j, a: (j ^ a[0], 0, 0))] * n_bits,
            out_specs=pl.BlockSpec((seg_len, 4 * HD), lambda j, a: (0, j)),
        ),
    )(at, wq, intra, *fars)

    if fast:
        weight_grad = reduce_weight(attn, dout, dout_pair, batch_index, seq_count)
    else:
        weight_grad = lax.psum_scatter(
            mm(attn, dout, 0, 0), ("seq", "batch"), scatter_dimension=0, tiled=True
        )

    if fast:
        far_half, far_wide = call(
            functools.partial(far_grad_four_body, 4), head_flops * n_bits, 4 * tok_bytes,
            out_shape=(sds(mats, BF), sds(mats, F32)),
            grid_spec=prefetch(
                num_scalar_prefetch=1, grid=(H // 4,),
                in_specs=[cols(4, n_bits), cols(4)], out_specs=(mat(4), mat(4)),
            ),
        )(seg_index.astype(jnp.int32)[None], wq, g)
        near = lax.ppermute(far_half, "seq", [(1, 0), (3, 2), (2, 3)])
        both = (far_wide + near.astype(F32)).astype(BF)
        got = [near, lax.ppermute(both, "seq", [(3, 1)]), lax.ppermute(both, "seq", [(3, 0)])]
        shares = jnp.stack([1 - bits[0], jnp.int32(1), jnp.int32(1)])
    else:
        far_half, far_wide = call(
            functools.partial(far_grad_body, n_bits, 4), head_flops * n_bits, 4 * tok_bytes,
            out_shape=(sds((n_bits,) + mats, BF), sds((n_bits,) + mats, F32)),
            grid=(H // 4,), in_specs=[cols(4, n_bits), cols(4)],
            out_specs=(stack(n_bits, 4),) * 2,
        )(wq, g)
        got = []
        pending_half, pending_wide = far_half, far_wide
        for b in range(n_bits):
            received = swapped(pending_half, "seq", 1 << b)
            got.append(received[0])
            if b + 1 < n_bits:
                pending_wide = pending_wide[1:] + received[1:].astype(F32)
                pending_half = pending_wide.astype(BF)
        shares = 1 - bits

    done = []
    for part in range(2):
        first = part * (H // 4)
        two = pl.BlockSpec((seg_len, 2 * HD), lambda h, *_, first=first: (0, h + first))
        two_mats = pl.BlockSpec((2, HD, HD), lambda h, *_, first=first: (h + first, 0, 0))
        two_blocks = pl.BlockSpec((n_blocks, 2, HD, HD), lambda h, *_, first=first: (0, h + first, 0, 0))
        done = call(
            functools.partial(main_body, n_bits, 2, first * 2, len(done)),
            5 * seg_len * TILE * width + head_flops * 2, 5 * tok_bytes,
            out_shape=(
                sds((seg_len, width), BF), sds((seg_len, width), F32), sds((seg_len, width), F32),
                sds((n_blocks,) + mats, F32), sds((seg_len, LEVELS * H), F32),
            ),
            grid_spec=prefetch(
                num_scalar_prefetch=1, grid=(H // 4,),
                in_specs=[two] * 4 + [whole_gain, two_blocks] + [two_mats] * n_bits
                + ([pl.BlockSpec(memory_space=pl.ANY)] * 4 + [whole_gain] if done else []),
                out_specs=(two, two, two, two_blocks, whole_gain),
                scratch_shapes=[pltpu.VMEM((seg_len, LEVELS * H), F32)],
            ),
            input_output_aliases={7 + n_bits + i: i for i in range(4)} if done else {},
        )(bits, q, k, v, g, gain, blocks, *fars, *done)
    query_grad, key_in, value_in, back, gain_grad = done

    key_grad, value_grad = call(
        functools.partial(final_body, 4), 2 * head_flops, 8 * tok_bytes,
        out_shape=(sds((seg_len, width), BF),) * 2,
        grid_spec=prefetch(
            num_scalar_prefetch=1, grid=(H // 4,),
            in_specs=[cols(4)] * 4 + [stack(n_blocks, 4)] + [mat(4)] * len(got),
            out_specs=(cols(4), cols(4)),
        ),
    )(shares, k, v, key_in, value_in, back, *got)
    return query_grad, key_grad, value_grad, gain_grad, weight_grad


def reduce_weight(attn, dout, dout_pair, batch_index, seq_count):
    seg_len, width = attn.shape
    quarter = width // 4
    core = batch_index & 1
    attn_pair = swapped(attn, "batch", 1)
    half = core.astype(jnp.int32)[None]

    def products(picks, dtype):
        lhs = pl.BlockSpec((seg_len, 4 * HD), lambda j, c: (0, j))
        grads = [pl.BlockSpec((seg_len, quarter), lambda j, c, n=n: (0, 2 * c[0] + n)) for n in (0, 0, 1, 1)]
        out = pl.BlockSpec((2 * HD, quarter), lambda j, c: (j, 0))
        return call(
            functools.partial(weight_body, picks), 4 * seg_len * width * quarter,
            2 * seg_len * (width + 2 * quarter) * 2 + width * quarter * 2,
            out_shape=(sds((width // 2, quarter), dtype),) * 2,
            grid_spec=pltpu.PrefetchScalarGridSpec(
                num_scalar_prefetch=1, grid=(width // (4 * HD),),
                in_specs=[lhs, lhs] + grads, out_specs=(out, out),
            ),
        )(half, attn, attn_pair, dout, dout_pair, dout, dout_pair)

    send_x, send_y = products(((1, 3), (2, 3)), BF)
    got_x = swapped(send_x, "batch", 2)
    got_y = swapped(send_y, "batch", 4)
    keep_x, keep_y = products(((0, 2), (0, 1)), F32)

    def pick(array, which):
        return array.reshape(seq_count, 2, HD, quarter)[:, which].astype(F32)

    send_xy = (pick(keep_x, 1) + pick(got_x, 1)).astype(BF)
    send_yx = (pick(keep_y, 1) + pick(got_y, 1)).astype(BF)
    got_xy = swapped(send_xy, "batch", 4)
    got_yx = swapped(send_yx, "batch", 2)
    left = pick(keep_x, 0) + pick(got_x, 0) + got_xy.astype(F32)
    right = pick(keep_y, 0) + pick(got_y, 0) + got_yx.astype(F32)
    total = jnp.concatenate([left, right], axis=2).reshape(2, 2, HD, width // 2)
    got_z = swapped(total[:, 1].astype(BF), "seq", 1).astype(F32)
    got_zz = swapped((total[1, 0] + got_z[1]).astype(BF), "seq", 2).astype(F32)
    mine = total[0, 0] + got_z[0] + got_zz
    rows = mine.shape[0] // 2
    other = swapped(lax.dynamic_slice_in_dim(mine, (1 - core) * rows, rows, 0), "batch", 1)
    own = lax.dynamic_slice_in_dim(mine, core * rows, rows, 0)
    return jnp.where(
        core == 0, jnp.concatenate([own, other], axis=1), jnp.concatenate([other, own], axis=1)
    )


def solution(mesh):
    row = P("batch", "seq", None)
    return jax.shard_map(
        local,
        mesh=mesh,
        in_specs=(row, row, row, row, P("batch", None), row),
        out_specs=(row, row, row, row, P(("seq", "batch"), None)),
        check_vma=False,
    )
```

```python
import functools

import jax
import jax.numpy as jnp
from jax import lax
from jax.experimental import pallas as pl
from jax.experimental.pallas import tpu as pltpu
from jax.sharding import PartitionSpec as P

H = 16
HD = 128
GROUP = 64
LEVELS = 8
HALF = 2 * GROUP
TILE = 4 * GROUP
SCALE = HD ** (-0.5)
EARLY = 60
BF = jnp.bfloat16
F32 = jnp.float32


def swapped(value, axis, mask):
    return lax.ppermute(value, axis, [(source, source ^ mask) for source in range(lax.axis_size(axis))])


def mm(a, b, ca, cb):
    return lax.dot_general(a, b, (((ca,), (cb,)), ((), ())), preferred_element_type=F32)


def call(body, flops, nbytes, vmem=16, **kwargs):
    return pl.pallas_call(
        body,
        cost_estimate=pl.CostEstimate(flops=int(flops), bytes_accessed=int(nbytes), transcendentals=0),
        compiler_params=pltpu.CompilerParams(vmem_limit_bytes=vmem * 1024 * 1024),
        **kwargs,
    )


def level_rows(gain_ref, head, levels):
    return {level: gain_ref[pl.ds(level * H + head, 1), :] for level in levels}


def half_masks():
    source = lax.broadcasted_iota(jnp.int32, (HALF, HALF), 0)
    target = lax.broadcasted_iota(jnp.int32, (HALF, HALF), 1)
    same = (source >= GROUP) == (target >= GROUP)
    return same & (source <= target), (source < GROUP) & (target >= GROUP)


def tile_weight(w, start, own, below):
    first, second = slice(start, start + HALF), slice(start + HALF, start + TILE)
    zero = jnp.zeros((HALF, HALF), F32)

    def corner(at):
        return jnp.where(own, w[0][:, at], jnp.where(below, w[1][:, at], 0.0))

    side = jnp.broadcast_to(w[2][:, second], (HALF, HALF))
    top = jnp.concatenate([corner(first), side], axis=1)
    bottom = jnp.concatenate([zero, corner(second)], axis=1)
    return jnp.concatenate([top, bottom], axis=0)


def far_blocks(seg_len):
    blocks = []
    size, level = TILE, 3
    while size < seg_len:
        for start in range(0, seg_len, 2 * size):
            blocks.append((level, start + size, start, size))
        size, level = 2 * size, level + 1
    return blocks


def states_body(k_ref, v_ref, wide_ref, half_ref, block_ref):
    seg_len = k_ref.shape[0]
    for i in range(wide_ref.shape[0]):
        cols = slice(i * HD, (i + 1) * HD)
        tiles = [
            mm(k_ref[start : start + TILE, cols], v_ref[start : start + TILE, cols], 0, 0)
            for start in range(0, seg_len, TILE)
        ]
        state = sum(tiles[1:], tiles[0])
        wide_ref[i] = state
        half_ref[i] = state.astype(BF)
        for j, (_, _, col, size) in enumerate(far_blocks(seg_len)):
            part = tiles[col // TILE : (col + size) // TILE]
            block_ref[j, i] = sum(part[1:], part[0]).astype(BF)


def intra_body(n_bits, heads, offset, bits_ref, q_ref, k_ref, v_ref, gain_ref, block_ref, *refs):
    out_ref, wq_ref, qt_ref = refs[-3:]
    seg_len = q_ref.shape[0]
    loc_bits = (seg_len // GROUP).bit_length() - 1
    own, below = half_masks()
    for i in range(heads):
        cols = slice(i * HD, (i + 1) * HD)
        w = level_rows(gain_ref, offset + pl.program_id(0) * heads + i, range(loc_bits + 1 + n_bits))
        qt = q_ref[:, cols].T
        qt_ref[cols] = qt
        for b in range(n_bits):
            factor = w[loc_bits + 1 + b] * bits_ref[b].astype(F32)
            at = (i * n_bits + b) * HD
            wq_ref[at : at + HD] = (qt.astype(F32) * factor).astype(BF)
        for start in range(0, seg_len, TILE):
            rows = slice(start, start + TILE)
            scores = mm(k_ref[rows, cols], qt[:, rows], 1, 0) * SCALE
            probs = (scores * tile_weight(w, start, own, below)).astype(BF)
            total = mm(v_ref[rows, cols].T, probs, 1, 0)
            for j, (level, row, _, size) in enumerate(far_blocks(seg_len)):
                if row <= start < row + size:
                    total += mm(block_ref[j, i], qt[:, rows], 0, 0) * (w[level][:, rows] * SCALE)
            out_ref[cols, rows] = total


def attn_body(n_bits, heads, at_ref, wq_ref, intra_ref, *refs):
    far_refs, out_ref = refs[:n_bits], refs[n_bits]
    for i in range(heads):
        cols = slice(i * HD, (i + 1) * HD)
        far = jnp.concatenate([ref[i] for ref in far_refs], axis=0)
        total = intra_ref[cols] + mm(far, wq_ref[i * n_bits * HD : (i + 1) * n_bits * HD], 0, 0) * SCALE
        place = pl.multiple_of((i ^ at_ref[1]) * HD, HD)
        out_ref[pl.ds(place, HD), :] = total.astype(BF)


def weight_body(picks, core_ref, attn_ref, attn2_ref, gx_ref, gx2_ref, gy_ref, gy2_ref, outx_ref, outy_ref):
    del core_ref
    for pick, left, right, out_ref in (
        (picks[0], gx_ref, gx2_ref, outx_ref),
        (picks[1], gy_ref, gy2_ref, outy_ref),
    ):
        total = 0.0
        for ref, grad_ref in ((attn_ref, left), (attn2_ref, right)):
            lhs = jnp.concatenate([ref[p * HD : (p + 1) * HD] for p in pick], axis=0)
            total += mm(lhs, grad_ref[...], 1, 0)
        out_ref[...] = total.astype(out_ref.dtype)


def attn_grad_body(count, at_ref, dout_ref, *refs):
    del at_ref
    out_ref = refs[-1]
    for j in range(count):
        @pl.when(pl.program_id(0) == j)
        def _(j=j):
            out_ref[...] = mm(refs[j][...], dout_ref[...], 1, 1).astype(BF)


def far_grad_body(n_bits, heads, wq_ref, g_ref, half_ref, wide_ref):
    for i in range(heads):
        span = n_bits * HD
        grad = mm(wq_ref[i * span : (i + 1) * span], g_ref[i * HD : (i + 1) * HD], 1, 1) * SCALE
        for b in range(n_bits):
            part = grad[b * HD : (b + 1) * HD]
            half_ref[b, i] = part.astype(BF)
            wide_ref[b, i] = part


def far_grad_four_body(heads, at_ref, wq_ref, g_ref, half_ref, wide_ref):
    for i in range(heads):
        grad = mm(wq_ref[2 * i * HD : 2 * (i + 1) * HD], g_ref[i * HD : (i + 1) * HD], 1, 1) * SCALE
        low, high = grad[:HD], grad[HD:]
        half_ref[i] = jnp.where(at_ref[0] == 3, high, low).astype(BF)
        wide_ref[i] = jnp.where(at_ref[0] == 3, low, high)


def main_body(n_bits, heads, offset, carried, bits_ref, qt_ref, k_ref, v_ref, g_ref, gain_ref, block_ref, *refs):
    far_refs = refs[:n_bits]
    gq_ref, gk_ref, gv_ref, back_ref, gain_grad_ref = refs[n_bits + carried :]
    seg_len = k_ref.shape[0]
    loc_bits = (seg_len // GROUP).bit_length() - 1
    own, below = half_masks()

    def down(x):
        return jnp.sum(x, axis=0, keepdims=True)

    for i in range(heads):
        head = offset + pl.program_id(0) * heads + i
        cols = slice(i * HD, (i + 1) * HD)
        w = level_rows(gain_ref, head, range(loc_bits + 1 + n_bits))
        far = jnp.concatenate([ref[i] for ref in far_refs], axis=0)

        gain_grad_ref[i] = jnp.zeros((LEVELS, seg_len), F32)

        def put(tokens, row, level, i=i):
            gain_grad_ref[i, level : level + 1, tokens] = row

        for start in range(0, seg_len, TILE):
            rows = slice(start, start + TILE)
            first, second = slice(start, start + HALF), slice(start + HALF, start + TILE)
            qt, gt = qt_ref[cols, rows], g_ref[cols, rows]
            qt_wide = qt.astype(F32)
            back = mm(far, gt, 1, 0)
            total = jnp.zeros((HD, TILE), F32)
            for b in range(n_bits):
                term = back[b * HD : (b + 1) * HD]
                bit = bits_ref[b].astype(F32)
                put(rows, down(qt_wide * term) * (SCALE * bit), loc_bits + 1 + b)
                total += term * (w[loc_bits + 1 + b][:, rows] * bit)
            for j, (level, row, _, size) in enumerate(far_blocks(seg_len)):
                if row <= start < row + size:
                    term = mm(block_ref[j, i], gt, 1, 0)
                    put(rows, down(qt_wide * term) * SCALE, level)
                    total += term * w[level][:, rows]
            weight = tile_weight(w, start, own, below)
            scores = mm(k_ref[rows, cols], qt, 1, 0) * SCALE
            prob_grad = mm(v_ref[rows, cols], gt, 1, 0)
            energy = scores * prob_grad
            for half, at in ((first, 0), (second, HALF)):
                corner = energy[at : at + HALF, at : at + HALF]
                put(half, down(jnp.where(own, corner, 0.0)), 0)
                put(half, down(jnp.where(below, corner, 0.0)), 1)
            put(second, down(energy[:HALF, HALF:]), 2)
            probs = (scores * weight).astype(BF)
            score_grad = (prob_grad * weight).astype(BF)
            total += mm(k_ref[rows, cols].T, score_grad, 1, 0)
            gq_ref[rows, cols] = (total * SCALE).astype(BF).T
            gk_ref[cols, rows] = mm(qt, score_grad, 1, 1) * SCALE
            gv_ref[cols, rows] = mm(gt, probs, 1, 1)
        for j, (level, row, _, size) in enumerate(far_blocks(seg_len)):
            rows = slice(row, row + size)
            weighted = (qt_ref[cols, rows].astype(F32) * w[level][:, rows]).astype(BF)
            back_ref[j, i] = mm(weighted, g_ref[cols, rows], 1, 1) * SCALE


def final_body(heads, gates, bits_ref, k_ref, v_ref, gk_ref, gv_ref, back_ref, *refs):
    got_refs, (key_ref, value_ref) = refs[:-3], refs[-2:]
    seg_len = k_ref.shape[0]
    for i in range(heads):
        cols = slice(i * HD, (i + 1) * HD)
        state = jnp.zeros((HD, HD), F32)
        for b, ref in enumerate(got_refs):
            part = ref[i].astype(F32)
            for bit in gates[b]:
                part = part * (1 - bits_ref[bit]).astype(F32)
            state += part
        for start in range(0, seg_len, TILE):
            rows = slice(start, start + TILE)
            here = state
            for j, (_, _, col, size) in enumerate(far_blocks(seg_len)):
                if col <= start < col + size:
                    here = here + back_ref[j, i]
            half = here.astype(BF)
            key = gk_ref[cols, rows] + mm(half, v_ref[rows, cols], 1, 1)
            value = gv_ref[cols, rows] + mm(half, k_ref[rows, cols], 0, 1)
            key_ref[rows, cols] = key.astype(BF).T
            value_ref[rows, cols] = value.astype(BF).T


def sds(shape, dtype):
    return jax.ShapeDtypeStruct(shape, dtype)


def local(queries, keys, values, level_gain, out_weight, out_grad):
    outs = step(queries[0], keys[0], values[0], level_gain[0], out_weight, out_grad[0])
    return tuple(x[None] for x in outs[:4]) + (outs[4],)


def is_fast(seq_count, batch_count):
    return batch_count == 8 and seq_count * batch_count == 2 * H


def step(q, k, v, gain, out_weight, dout):
    seg_len, width = q.shape
    seq_count, batch_count = lax.axis_size("seq"), lax.axis_size("batch")
    n_bits = seq_count.bit_length() - 1
    seg_index, batch_index = lax.axis_index("seq"), lax.axis_index("batch")
    bits = jnp.stack([seg_index >> b & 1 for b in range(n_bits)]).astype(jnp.int32)
    fast = is_fast(seq_count, batch_count)
    prefetch = pltpu.PrefetchScalarGridSpec
    tok_bytes = seg_len * width * 2
    head_flops = 2 * seg_len * HD * HD * H
    n_blocks = len(far_blocks(seg_len))
    mats = (H, HD, HD)

    def cols(heads, scale=1):
        return pl.BlockSpec((seg_len, heads * HD * scale), lambda h, *_: (0, h))

    def turned(heads, scale=1):
        return pl.BlockSpec((heads * HD * scale, seg_len), lambda h, *_: (h, 0))

    def mat(heads):
        return pl.BlockSpec((heads, HD, HD), lambda h, *_: (h, 0, 0))

    def stack(count, heads):
        return pl.BlockSpec((count, heads, HD, HD), lambda h, *_: (0, h, 0, 0))

    whole_gain = pl.BlockSpec((LEVELS * H, seg_len), lambda h, *_: (0, 0))
    gain = gain.T

    state_wide, state_half, blocks = call(
        states_body, head_flops, 2 * tok_bytes, EARLY,
        out_shape=(sds(mats, F32), sds(mats, BF), sds((n_blocks,) + mats, BF)),
        grid=(H // 4,), in_specs=[cols(4), cols(4)],
        out_specs=(mat(4), mat(4), stack(n_blocks, 4)),
    )(k, v)
    fars = []
    running_wide, running = state_wide, state_half
    for b in range(n_bits):
        received = swapped(running, "seq", 1 << b)
        fars.append(received)
        if b + 1 < n_bits:
            running_wide = running_wide + received.astype(F32)
            running = running_wide.astype(BF)

    if fast:
        pieces = {0: out_weight}
        dout_pair = swapped(dout, "batch", 1)
        pieces[2] = swapped(out_weight, "batch", 2)
        pieces[4] = swapped(out_weight, "batch", 4)
        pieces[1] = swapped(out_weight, "batch", 1)
        pieces[3] = swapped(pieces[2], "batch", 1)
        pieces[5] = swapped(pieces[4], "batch", 1)
        pieces[6] = swapped(out_weight, "batch", 6)
        pieces[7] = swapped(pieces[6], "batch", 1)
        stages = [[(pieces[m], batch_index ^ m) for m in group] for group in ((0, 1), (2, 4, 3, 5), (6, 7))]
        g = None
        for stage in stages:
            count, piece_rows = len(stage), stage[0][0].shape[0]
            index = jnp.stack([at for _, at in stage]).astype(jnp.int32)
            arrays = [array for array, _ in stage]
            extra = [] if g is None else [g]
            g = call(
                functools.partial(attn_grad_body, count),
                2 * seg_len * width * piece_rows * count, tok_bytes + count * piece_rows * (width + seg_len) * 2, 30,
                out_shape=pltpu.HBM((width, seg_len), BF),
                grid_spec=prefetch(
                    num_scalar_prefetch=1, grid=(count,),
                    in_specs=[pl.BlockSpec((seg_len, width), lambda j, at: (0, 0))]
                    + [pl.BlockSpec((piece_rows, width), lambda j, at: (0, 0))] * count
                    + [pl.BlockSpec(memory_space=pl.ANY)] * len(extra),
                    out_specs=pl.BlockSpec((piece_rows, seg_len), lambda j, at: (at[j], 0)),
                ),
                input_output_aliases={} if g is None else {2 + count: 0},
            )(index, dout, *arrays, *extra)
    else:
        gathered = lax.all_gather(out_weight, "batch", axis=0, tiled=True)
        g = mm(gathered, dout, 1, 1).astype(BF)

    formed = []
    for part in range(2):
        first = part * (H // 8)
        four = pl.BlockSpec((seg_len, 4 * HD), lambda h, *_, first=first: (0, h + first))
        four_turned = pl.BlockSpec((4 * HD, seg_len), lambda h, *_, first=first: (h + first, 0))
        four_wide = pl.BlockSpec((4 * HD * n_bits, seg_len), lambda h, *_, first=first: (h + first, 0))
        four_blocks = pl.BlockSpec((n_blocks, 4, HD, HD), lambda h, *_, first=first: (0, h + first, 0, 0))
        formed = call(
            functools.partial(intra_body, n_bits, 4, first * 4),
            2 * seg_len * TILE * width, 5 * tok_bytes, EARLY,
            out_shape=(sds((width, seg_len), F32), sds((n_bits * width, seg_len), BF), sds((width, seg_len), BF)),
            grid_spec=prefetch(
                num_scalar_prefetch=1, grid=(H // 8,),
                in_specs=[four, four, four, whole_gain, four_blocks]
                + [pl.BlockSpec(memory_space=pl.ANY)] * len(formed),
                out_specs=(four_turned, four_wide, four_turned),
            ),
            input_output_aliases={6 + i: i for i in range(3)} if formed else {},
        )(bits, q, k, v, gain, blocks, *formed)
    intra, wq, qt = formed

    at = jnp.stack([seg_index, batch_index >> 1]).astype(jnp.int32)
    if not fast:
        at = jnp.zeros_like(at)
    attn = call(
        functools.partial(attn_body, n_bits, 4), head_flops * n_bits, 5 * tok_bytes,
        out_shape=sds((width, seg_len), BF),
        grid_spec=prefetch(
            num_scalar_prefetch=1, grid=(H // 4,),
            in_specs=[
                pl.BlockSpec((4 * HD * n_bits, seg_len), lambda j, a: (j ^ a[0], 0)),
                pl.BlockSpec((4 * HD, seg_len), lambda j, a: (j ^ a[0], 0)),
            ]
            + [pl.BlockSpec((4, HD, HD), lambda j, a: (j ^ a[0], 0, 0))] * n_bits,
            out_specs=pl.BlockSpec((4 * HD, seg_len), lambda j, a: (j, 0)),
        ),
    )(at, wq, intra, *fars)

    if fast:
        weight_grad = reduce_weight(attn, dout, dout_pair, batch_index, seq_count)
    else:
        weight_grad = lax.psum_scatter(
            mm(attn, dout, 1, 0), ("seq", "batch"), scatter_dimension=0, tiled=True
        )

    if fast:
        far_half, far_wide = call(
            functools.partial(far_grad_four_body, 4), head_flops * n_bits, 4 * tok_bytes,
            out_shape=(sds(mats, BF), sds(mats, F32)),
            grid_spec=prefetch(
                num_scalar_prefetch=1, grid=(H // 4,),
                in_specs=[turned(4, n_bits), turned(4)], out_specs=(mat(4), mat(4)),
            ),
        )(seg_index.astype(jnp.int32)[None], wq, g)
        near = lax.ppermute(far_half, "seq", [(1, 0), (3, 2)])
        both = (far_wide + near.astype(F32)).astype(BF)
        got = [near, lax.ppermute(both, "seq", [(2, 0)]), lax.ppermute(both, "seq", [(2, 1), (3, 2)])]
        gates = ((0, 1), (), ())
    else:
        far_half, far_wide = call(
            functools.partial(far_grad_body, n_bits, 4), head_flops * n_bits, 4 * tok_bytes,
            out_shape=(sds((n_bits,) + mats, BF), sds((n_bits,) + mats, F32)),
            grid=(H // 4,), in_specs=[turned(4, n_bits), turned(4)],
            out_specs=(stack(n_bits, 4),) * 2,
        )(wq, g)
        got = []
        pending_half, pending_wide = far_half, far_wide
        for b in range(n_bits):
            received = swapped(pending_half, "seq", 1 << b)
            got.append(received[0])
            if b + 1 < n_bits:
                pending_wide = pending_wide[1:] + received[1:].astype(F32)
                pending_half = pending_wide.astype(BF)
        gates = tuple((b,) for b in range(n_bits))

    done = []
    bounds = (0, H // 8, 3 * H // 8, H // 2)
    for first, last in zip(bounds, bounds[1:]):
        two = pl.BlockSpec((seg_len, 2 * HD), lambda h, *_, first=first: (0, h + first))
        two_turned = pl.BlockSpec((2 * HD, seg_len), lambda h, *_, first=first: (h + first, 0))
        two_mats = pl.BlockSpec((2, HD, HD), lambda h, *_, first=first: (h + first, 0, 0))
        two_blocks = pl.BlockSpec((n_blocks, 2, HD, HD), lambda h, *_, first=first: (0, h + first, 0, 0))
        two_levels = pl.BlockSpec((2, LEVELS, seg_len), lambda h, *_, first=first: (h + first, 0, 0))
        done = call(
            functools.partial(main_body, n_bits, 2, first * 2, len(done)),
            (5 * seg_len * TILE * width + head_flops * 2) * (last - first) // 4, 5 * tok_bytes * (last - first) // 4,
            out_shape=(
                sds((seg_len, width), BF), pltpu.HBM((width, seg_len), F32), pltpu.HBM((width, seg_len), F32),
                pltpu.HBM((n_blocks,) + mats, F32), sds((H, LEVELS, seg_len), F32),
            ),
            grid_spec=prefetch(
                num_scalar_prefetch=1, grid=(last - first,),
                in_specs=[two_turned, two, two, two_turned, whole_gain, two_blocks] + [two_mats] * n_bits
                + ([pl.BlockSpec(memory_space=pl.ANY)] * 5 if done else []),
                out_specs=(two, two_turned, two_turned, two_blocks, two_levels),
            ),
            input_output_aliases={7 + n_bits + i: i for i in range(5)} if done else {},
        )(bits, qt, k, v, g, gain, blocks, *fars, *done)
    query_grad, key_in, value_in, back, gain_grad = done

    gain_grad = gain_grad.transpose(2, 1, 0).reshape(seg_len, LEVELS * H)
    key_grad, value_grad = call(
        functools.partial(final_body, 4, gates), 2 * head_flops, 8 * tok_bytes, 56,
        out_shape=(sds((seg_len, width), BF),) * 2,
        grid_spec=prefetch(
            num_scalar_prefetch=1, grid=(H // 4,),
            in_specs=[cols(4)] * 2 + [turned(4)] * 2 + [stack(n_blocks, 4)] + [mat(4)] * len(got)
            + [pl.BlockSpec(memory_space=pl.ANY)],
            out_specs=(cols(4), cols(4)),
        ),
    )(bits, k, v, key_in, value_in, back, *got, gain_grad)
    return query_grad, key_grad, value_grad, gain_grad, weight_grad


def reduce_weight(attn, dout, dout_pair, batch_index, seq_count):
    width, seg_len = attn.shape
    quarter = width // 4
    core = batch_index & 1
    attn_pair = swapped(attn, "batch", 1)
    half = core.astype(jnp.int32)[None]

    def products(picks, dtype):
        lhs = pl.BlockSpec((4 * HD, seg_len), lambda j, c: (j, 0))
        grads = [pl.BlockSpec((seg_len, quarter), lambda j, c, n=n: (0, 2 * c[0] + n)) for n in (0, 0, 1, 1)]
        out = pl.BlockSpec((2 * HD, quarter), lambda j, c: (j, 0))
        return call(
            functools.partial(weight_body, picks), 4 * seg_len * width * quarter,
            2 * seg_len * (width + 2 * quarter) * 2 + width * quarter * 2,
            out_shape=(sds((width // 2, quarter), dtype),) * 2,
            grid_spec=pltpu.PrefetchScalarGridSpec(
                num_scalar_prefetch=1, grid=(width // (4 * HD),),
                in_specs=[lhs, lhs] + grads, out_specs=(out, out),
            ),
        )(half, attn, attn_pair, dout, dout_pair, dout, dout_pair)

    send_x, send_y = products(((1, 3), (2, 3)), BF)
    got_x = swapped(send_x, "batch", 2)
    got_y = swapped(send_y, "batch", 4)
    keep_x, keep_y = products(((0, 2), (0, 1)), F32)

    def pick(array, which):
        return array.reshape(seq_count, 2, HD, quarter)[:, which].astype(F32)

    send_xy = (pick(keep_x, 1) + pick(got_x, 1)).astype(BF)
    send_yx = (pick(keep_y, 1) + pick(got_y, 1)).astype(BF)
    got_xy = swapped(send_xy, "batch", 4)
    got_yx = swapped(send_yx, "batch", 2)
    left = pick(keep_x, 0) + pick(got_x, 0) + got_xy.astype(F32)
    right = pick(keep_y, 0) + pick(got_y, 0) + got_yx.astype(F32)
    total = jnp.concatenate([left, right], axis=2).reshape(2, 2, HD, width // 2)
    got_z = swapped(total[:, 1].astype(BF), "seq", 1)
    got_zz = swapped((total[1, 0] + got_z[1].astype(F32)).astype(BF), "seq", 2)
    mine = total[0, 0] + got_z[0].astype(F32) + got_zz.astype(F32)
    rows = mine.shape[0] // 2
    other = swapped(lax.dynamic_slice_in_dim(mine, (1 - core) * rows, rows, 0), "batch", 1)
    own = lax.dynamic_slice_in_dim(mine, core * rows, rows, 0)
    return jnp.where(
        core == 0, jnp.concatenate([own, other], axis=1), jnp.concatenate([other, own], axis=1)
    )


def solution(mesh):
    row = P("batch", "seq", None)
    return jax.shard_map(
        local,
        mesh=mesh,
        in_specs=(row, row, row, row, P("batch", None), row),
        out_specs=(row, row, row, row, P(("seq", "batch"), None)),
        check_vma=False,
    )
```

```python
import functools

import jax
import jax.numpy as jnp
from jax import lax
from jax.experimental import pallas as pl
from jax.experimental.pallas import tpu as pltpu
from jax.sharding import PartitionSpec as P

H = 16
HD = 128
GROUP = 64
LEVELS = 8
HALF = 2 * GROUP
TILE = 4 * GROUP
SCALE = HD ** (-0.5)
EARLY = 60
BF = jnp.bfloat16
F32 = jnp.float32


def swapped(value, axis, mask):
    return lax.ppermute(value, axis, [(source, source ^ mask) for source in range(lax.axis_size(axis))])


def mm(a, b, ca, cb):
    return lax.dot_general(a, b, (((ca,), (cb,)), ((), ())), preferred_element_type=F32)


def call(body, flops, nbytes, vmem=16, **kwargs):
    return pl.pallas_call(
        body,
        cost_estimate=pl.CostEstimate(flops=int(flops), bytes_accessed=int(nbytes), transcendentals=0),
        compiler_params=pltpu.CompilerParams(vmem_limit_bytes=vmem * 1024 * 1024),
        **kwargs,
    )


def level_rows(gain_ref, head, levels):
    return {level: gain_ref[pl.ds(level * H + head, 1), :] for level in levels}


def half_masks():
    source = lax.broadcasted_iota(jnp.int32, (HALF, HALF), 0)
    target = lax.broadcasted_iota(jnp.int32, (HALF, HALF), 1)
    same = (source >= GROUP) == (target >= GROUP)
    return same & (source <= target), (source < GROUP) & (target >= GROUP)


def tile_weight(w, start, own, below):
    first, second = slice(start, start + HALF), slice(start + HALF, start + TILE)
    zero = jnp.zeros((HALF, HALF), F32)

    def corner(at):
        return jnp.where(own, w[0][:, at], jnp.where(below, w[1][:, at], 0.0))

    side = jnp.broadcast_to(w[2][:, second], (HALF, HALF))
    top = jnp.concatenate([corner(first), side], axis=1)
    bottom = jnp.concatenate([zero, corner(second)], axis=1)
    return jnp.concatenate([top, bottom], axis=0)


def far_blocks(seg_len):
    blocks = []
    size, level = TILE, 3
    while size < seg_len:
        for start in range(0, seg_len, 2 * size):
            blocks.append((level, start + size, start, size))
        size, level = 2 * size, level + 1
    return blocks


def states_body(k_ref, v_ref, half_ref, block_ref):
    seg_len = k_ref.shape[0]
    for i in range(half_ref.shape[0]):
        cols = slice(i * HD, (i + 1) * HD)
        tiles = [
            mm(k_ref[start : start + TILE, cols], v_ref[start : start + TILE, cols], 0, 0)
            for start in range(0, seg_len, TILE)
        ]
        half_ref[i] = sum(tiles[1:], tiles[0]).astype(BF)
        for j, (_, _, col, size) in enumerate(far_blocks(seg_len)):
            part = tiles[col // TILE : (col + size) // TILE]
            block_ref[j, i] = sum(part[1:], part[0]).astype(BF)


def intra_body(n_bits, heads, offset, bits_ref, q_ref, k_ref, v_ref, gain_ref, block_ref, *refs):
    out_ref, wq_ref, qt_ref = refs[-3:]
    seg_len = q_ref.shape[0]
    loc_bits = (seg_len // GROUP).bit_length() - 1
    own, below = half_masks()
    for i in range(heads):
        cols = slice(i * HD, (i + 1) * HD)
        w = level_rows(gain_ref, offset + pl.program_id(0) * heads + i, range(loc_bits + 1 + n_bits))
        qt = q_ref[:, cols].T
        qt_ref[cols] = qt
        for b in range(n_bits):
            factor = w[loc_bits + 1 + b] * bits_ref[b].astype(F32)
            at = (i * n_bits + b) * HD
            wq_ref[at : at + HD] = (qt.astype(F32) * factor).astype(BF)
        for start in range(0, seg_len, TILE):
            rows = slice(start, start + TILE)
            scores = mm(k_ref[rows, cols], qt[:, rows], 1, 0) * SCALE
            probs = (scores * tile_weight(w, start, own, below)).astype(BF)
            total = mm(v_ref[rows, cols].T, probs, 1, 0)
            for j, (level, row, _, size) in enumerate(far_blocks(seg_len)):
                if row <= start < row + size:
                    total += mm(block_ref[j, i], qt[:, rows], 0, 0) * (w[level][:, rows] * SCALE)
            out_ref[cols, rows] = total


def attn_body(n_bits, heads, at_ref, wq_ref, intra_ref, *refs):
    far_refs, out_ref = refs[:n_bits], refs[n_bits]
    for i in range(heads):
        cols = slice(i * HD, (i + 1) * HD)
        far = jnp.concatenate([ref[i] for ref in far_refs], axis=0)
        total = intra_ref[cols] + mm(far, wq_ref[i * n_bits * HD : (i + 1) * n_bits * HD], 0, 0) * SCALE
        place = pl.multiple_of((i ^ at_ref[1]) * HD, HD)
        out_ref[pl.ds(place, HD), :] = total.astype(BF)


def weight_body(picks, core_ref, attn_ref, attn2_ref, gx_ref, gx2_ref, gy_ref, gy2_ref, outx_ref, outy_ref):
    del core_ref
    for pick, left, right, out_ref in (
        (picks[0], gx_ref, gx2_ref, outx_ref),
        (picks[1], gy_ref, gy2_ref, outy_ref),
    ):
        total = 0.0
        for ref, grad_ref in ((attn_ref, left), (attn2_ref, right)):
            lhs = jnp.concatenate([ref[p * HD : (p + 1) * HD] for p in pick], axis=0)
            total += mm(lhs, grad_ref[...], 1, 0)
        out_ref[...] = total.astype(out_ref.dtype)


def attn_grad_body(count, at_ref, dout_ref, *refs):
    del at_ref
    out_ref = refs[-1]
    for j in range(count):
        @pl.when(pl.program_id(0) == j)
        def _(j=j):
            out_ref[...] = mm(refs[j][...], dout_ref[...], 1, 1).astype(BF)


def far_grad_body(n_bits, heads, wq_ref, g_ref, half_ref, wide_ref):
    for i in range(heads):
        span = n_bits * HD
        grad = mm(wq_ref[i * span : (i + 1) * span], g_ref[i * HD : (i + 1) * HD], 1, 1) * SCALE
        for b in range(n_bits):
            part = grad[b * HD : (b + 1) * HD]
            half_ref[b, i] = part.astype(BF)
            wide_ref[b, i] = part


def far_grad_four_body(heads, at_ref, wq_ref, g_ref, half_ref, wide_ref):
    for i in range(heads):
        grad = mm(wq_ref[2 * i * HD : 2 * (i + 1) * HD], g_ref[i * HD : (i + 1) * HD], 1, 1) * SCALE
        low, high = grad[:HD], grad[HD:]
        half_ref[i] = jnp.where(at_ref[0] == 3, high, low).astype(BF)
        wide_ref[i] = jnp.where(at_ref[0] == 3, low, high)


def main_body(n_bits, heads, offset, carried, bits_ref, qt_ref, k_ref, v_ref, g_ref, gain_ref, block_ref, *refs):
    far_refs = refs[:n_bits]
    gq_ref, gk_ref, gv_ref, back_ref, gain_grad_ref = refs[n_bits + carried :]
    seg_len = k_ref.shape[0]
    loc_bits = (seg_len // GROUP).bit_length() - 1
    own, below = half_masks()

    def down(x):
        return jnp.sum(x, axis=0, keepdims=True)

    for i in range(heads):
        head = offset + pl.program_id(0) * heads + i
        cols = slice(i * HD, (i + 1) * HD)
        w = level_rows(gain_ref, head, range(loc_bits + 1 + n_bits))
        far = jnp.concatenate([ref[i] for ref in far_refs], axis=0)

        gain_grad_ref[i] = jnp.zeros((LEVELS, seg_len), F32)

        def put(tokens, row, level, i=i):
            gain_grad_ref[i, level : level + 1, tokens] = row

        for start in range(0, seg_len, TILE):
            rows = slice(start, start + TILE)
            first, second = slice(start, start + HALF), slice(start + HALF, start + TILE)
            qt, gt = qt_ref[cols, rows], g_ref[cols, rows]
            qt_wide = qt.astype(F32)
            back = mm(far, gt, 1, 0)
            total = jnp.zeros((HD, TILE), F32)
            for b in range(n_bits):
                term = back[b * HD : (b + 1) * HD]
                bit = bits_ref[b].astype(F32)
                put(rows, down(qt_wide * term) * (SCALE * bit), loc_bits + 1 + b)
                total += term * (w[loc_bits + 1 + b][:, rows] * bit)
            for j, (level, row, _, size) in enumerate(far_blocks(seg_len)):
                if row <= start < row + size:
                    term = mm(block_ref[j, i], gt, 1, 0)
                    put(rows, down(qt_wide * term) * SCALE, level)
                    total += term * w[level][:, rows]
            weight = tile_weight(w, start, own, below)
            scores = mm(k_ref[rows, cols], qt, 1, 0) * SCALE
            prob_grad = mm(v_ref[rows, cols], gt, 1, 0)
            energy = scores * prob_grad
            for half, at in ((first, 0), (second, HALF)):
                corner = energy[at : at + HALF, at : at + HALF]
                put(half, down(jnp.where(own, corner, 0.0)), 0)
                put(half, down(jnp.where(below, corner, 0.0)), 1)
            put(second, down(energy[:HALF, HALF:]), 2)
            probs = (scores * weight).astype(BF)
            score_grad = (prob_grad * weight).astype(BF)
            total += mm(k_ref[rows, cols].T, score_grad, 1, 0)
            gq_ref[rows, cols] = (total * SCALE).astype(BF).T
            gk_ref[cols, rows] = mm(qt, score_grad, 1, 1) * SCALE
            gv_ref[cols, rows] = mm(gt, probs, 1, 1)
        for j, (level, row, _, size) in enumerate(far_blocks(seg_len)):
            rows = slice(row, row + size)
            weighted = (qt_ref[cols, rows].astype(F32) * w[level][:, rows]).astype(BF)
            back_ref[j, i] = mm(weighted, g_ref[cols, rows], 1, 1) * SCALE


def final_body(heads, gates, bits_ref, k_ref, v_ref, gk_ref, gv_ref, back_ref, *refs):
    got_refs, (key_ref, value_ref) = refs[:-3], refs[-2:]
    seg_len = k_ref.shape[0]
    for i in range(heads):
        cols = slice(i * HD, (i + 1) * HD)
        state = jnp.zeros((HD, HD), F32)
        for b, ref in enumerate(got_refs):
            part = ref[i].astype(F32)
            for bit in gates[b]:
                part = part * (1 - bits_ref[bit]).astype(F32)
            state += part
        for start in range(0, seg_len, TILE):
            rows = slice(start, start + TILE)
            here = state
            for j, (_, _, col, size) in enumerate(far_blocks(seg_len)):
                if col <= start < col + size:
                    here = here + back_ref[j, i]
            half = here.astype(BF)
            key = gk_ref[cols, rows] + mm(half, v_ref[rows, cols], 1, 1)
            value = gv_ref[cols, rows] + mm(half, k_ref[rows, cols], 0, 1)
            key_ref[rows, cols] = key.astype(BF).T
            value_ref[rows, cols] = value.astype(BF).T


def sds(shape, dtype):
    return jax.ShapeDtypeStruct(shape, dtype)


def local(queries, keys, values, level_gain, out_weight, out_grad):
    outs = step(queries[0], keys[0], values[0], level_gain[0], out_weight, out_grad[0])
    return tuple(x[None] for x in outs[:4]) + (outs[4],)


def is_fast(seq_count, batch_count):
    return batch_count == 8 and seq_count * batch_count == 2 * H


def step(q, k, v, gain, out_weight, dout):
    seg_len, width = q.shape
    seq_count, batch_count = lax.axis_size("seq"), lax.axis_size("batch")
    n_bits = seq_count.bit_length() - 1
    seg_index, batch_index = lax.axis_index("seq"), lax.axis_index("batch")
    bits = jnp.stack([seg_index >> b & 1 for b in range(n_bits)]).astype(jnp.int32)
    fast = is_fast(seq_count, batch_count)
    prefetch = pltpu.PrefetchScalarGridSpec
    tok_bytes = seg_len * width * 2
    head_flops = 2 * seg_len * HD * HD * H
    n_blocks = len(far_blocks(seg_len))
    mats = (H, HD, HD)

    def cols(heads, scale=1):
        return pl.BlockSpec((seg_len, heads * HD * scale), lambda h, *_: (0, h))

    def turned(heads, scale=1):
        return pl.BlockSpec((heads * HD * scale, seg_len), lambda h, *_: (h, 0))

    def mat(heads):
        return pl.BlockSpec((heads, HD, HD), lambda h, *_: (h, 0, 0))

    def stack(count, heads):
        return pl.BlockSpec((count, heads, HD, HD), lambda h, *_: (0, h, 0, 0))

    whole_gain = pl.BlockSpec((LEVELS * H, seg_len), lambda h, *_: (0, 0))
    gain = gain.T

    state_half, blocks = call(
        states_body, head_flops, 2 * tok_bytes, EARLY,
        out_shape=(sds(mats, BF), sds((n_blocks,) + mats, BF)),
        grid=(H // 4,), in_specs=[cols(4), cols(4)],
        out_specs=(mat(4), stack(n_blocks, 4)),
    )(k, v)
    fars = []
    running = state_half
    for b in range(n_bits):
        received = swapped(running, "seq", 1 << b)
        fars.append(received)
        if b + 1 < n_bits:
            running = (running.astype(F32) + received.astype(F32)).astype(BF)

    if fast:
        pieces = {0: out_weight}
        dout_pair = swapped(dout, "batch", 1)
        pieces[2] = swapped(out_weight, "batch", 2)
        pieces[4] = swapped(out_weight, "batch", 4)
        pieces[1] = swapped(out_weight, "batch", 1)
        pieces[3] = swapped(pieces[2], "batch", 1)
        pieces[5] = swapped(pieces[4], "batch", 1)
        pieces[6] = swapped(out_weight, "batch", 6)
        pieces[7] = swapped(pieces[6], "batch", 1)
        stages = [[(pieces[m], batch_index ^ m) for m in group] for group in ((0, 1), (2, 4), (3, 5), (6, 7))]
        g = None
        for stage in stages:
            count, piece_rows = len(stage), stage[0][0].shape[0]
            index = jnp.stack([at for _, at in stage]).astype(jnp.int32)
            arrays = [array for array, _ in stage]
            extra = [] if g is None else [g]
            g = call(
                functools.partial(attn_grad_body, count),
                2 * seg_len * width * piece_rows * count, tok_bytes + count * piece_rows * (width + seg_len) * 2, 30,
                out_shape=pltpu.HBM((width, seg_len), BF),
                grid_spec=prefetch(
                    num_scalar_prefetch=1, grid=(count,),
                    in_specs=[pl.BlockSpec((seg_len, width), lambda j, at: (0, 0))]
                    + [pl.BlockSpec((piece_rows, width), lambda j, at: (0, 0))] * count
                    + [pl.BlockSpec(memory_space=pl.ANY)] * len(extra),
                    out_specs=pl.BlockSpec((piece_rows, seg_len), lambda j, at: (at[j], 0)),
                ),
                input_output_aliases={} if g is None else {2 + count: 0},
            )(index, dout, *arrays, *extra)
    else:
        gathered = lax.all_gather(out_weight, "batch", axis=0, tiled=True)
        g = mm(gathered, dout, 1, 1).astype(BF)

    formed = []
    for part in range(2):
        first = part * (H // 8)
        four = pl.BlockSpec((seg_len, 4 * HD), lambda h, *_, first=first: (0, h + first))
        four_turned = pl.BlockSpec((4 * HD, seg_len), lambda h, *_, first=first: (h + first, 0))
        four_wide = pl.BlockSpec((4 * HD * n_bits, seg_len), lambda h, *_, first=first: (h + first, 0))
        four_blocks = pl.BlockSpec((n_blocks, 4, HD, HD), lambda h, *_, first=first: (0, h + first, 0, 0))
        formed = call(
            functools.partial(intra_body, n_bits, 4, first * 4),
            2 * seg_len * TILE * width, 5 * tok_bytes, EARLY,
            out_shape=(sds((width, seg_len), F32), sds((n_bits * width, seg_len), BF), sds((width, seg_len), BF)),
            grid_spec=prefetch(
                num_scalar_prefetch=1, grid=(H // 8,),
                in_specs=[four, four, four, whole_gain, four_blocks]
                + [pl.BlockSpec(memory_space=pl.ANY)] * len(formed),
                out_specs=(four_turned, four_wide, four_turned),
            ),
            input_output_aliases={6 + i: i for i in range(3)} if formed else {},
        )(bits, q, k, v, gain, blocks, *formed)
    intra, wq, qt = formed

    at = jnp.stack([seg_index, batch_index >> 1]).astype(jnp.int32)
    if not fast:
        at = jnp.zeros_like(at)
    attn = call(
        functools.partial(attn_body, n_bits, 4), head_flops * n_bits, 5 * tok_bytes,
        out_shape=sds((width, seg_len), BF),
        grid_spec=prefetch(
            num_scalar_prefetch=1, grid=(H // 4,),
            in_specs=[
                pl.BlockSpec((4 * HD * n_bits, seg_len), lambda j, a: (j ^ a[0], 0)),
                pl.BlockSpec((4 * HD, seg_len), lambda j, a: (j ^ a[0], 0)),
            ]
            + [pl.BlockSpec((4, HD, HD), lambda j, a: (j ^ a[0], 0, 0))] * n_bits,
            out_specs=pl.BlockSpec((4 * HD, seg_len), lambda j, a: (j, 0)),
        ),
    )(at, wq, intra, *fars)

    if fast:
        weight_grad = reduce_weight(attn, dout, dout_pair, batch_index, seq_count)
    else:
        weight_grad = lax.psum_scatter(
            mm(attn, dout, 1, 0), ("seq", "batch"), scatter_dimension=0, tiled=True
        )

    if fast:
        far_half, far_wide = call(
            functools.partial(far_grad_four_body, 4), head_flops * n_bits, 4 * tok_bytes,
            out_shape=(sds(mats, BF), sds(mats, F32)),
            grid_spec=prefetch(
                num_scalar_prefetch=1, grid=(H // 4,),
                in_specs=[turned(4, n_bits), turned(4)], out_specs=(mat(4), mat(4)),
            ),
        )(seg_index.astype(jnp.int32)[None], wq, g)
        near = lax.ppermute(far_half, "seq", [(1, 0), (3, 2)])
        both = (far_wide + near.astype(F32)).astype(BF)
        got = [near, lax.ppermute(both, "seq", [(2, 0)]), lax.ppermute(both, "seq", [(2, 1), (3, 2)])]
        gates = ((0, 1), (), ())
    else:
        far_half, far_wide = call(
            functools.partial(far_grad_body, n_bits, 4), head_flops * n_bits, 4 * tok_bytes,
            out_shape=(sds((n_bits,) + mats, BF), sds((n_bits,) + mats, F32)),
            grid=(H // 4,), in_specs=[turned(4, n_bits), turned(4)],
            out_specs=(stack(n_bits, 4),) * 2,
        )(wq, g)
        got = []
        pending_half, pending_wide = far_half, far_wide
        for b in range(n_bits):
            received = swapped(pending_half, "seq", 1 << b)
            got.append(received[0])
            if b + 1 < n_bits:
                pending_wide = pending_wide[1:] + received[1:].astype(F32)
                pending_half = pending_wide.astype(BF)
        gates = tuple((b,) for b in range(n_bits))

    done = []
    bounds = (0, H // 16, 5 * H // 16, H // 2)
    for first, last in zip(bounds, bounds[1:]):
        two = pl.BlockSpec((seg_len, 2 * HD), lambda h, *_, first=first: (0, h + first))
        two_turned = pl.BlockSpec((2 * HD, seg_len), lambda h, *_, first=first: (h + first, 0))
        two_mats = pl.BlockSpec((2, HD, HD), lambda h, *_, first=first: (h + first, 0, 0))
        two_blocks = pl.BlockSpec((n_blocks, 2, HD, HD), lambda h, *_, first=first: (0, h + first, 0, 0))
        two_levels = pl.BlockSpec((2, LEVELS, seg_len), lambda h, *_, first=first: (h + first, 0, 0))
        done = call(
            functools.partial(main_body, n_bits, 2, first * 2, len(done)),
            (5 * seg_len * TILE * width + head_flops * 2) * (last - first) // 4, 5 * tok_bytes * (last - first) // 4,
            out_shape=(
                sds((seg_len, width), BF), pltpu.HBM((width, seg_len), F32), pltpu.HBM((width, seg_len), F32),
                pltpu.HBM((n_blocks,) + mats, F32), sds((H, LEVELS, seg_len), F32),
            ),
            grid_spec=prefetch(
                num_scalar_prefetch=1, grid=(last - first,),
                in_specs=[two_turned, two, two, two_turned, whole_gain, two_blocks] + [two_mats] * n_bits
                + ([pl.BlockSpec(memory_space=pl.ANY)] * 5 if done else []),
                out_specs=(two, two_turned, two_turned, two_blocks, two_levels),
            ),
            input_output_aliases={7 + n_bits + i: i for i in range(5)} if done else {},
        )(bits, qt, k, v, g, gain, blocks, *fars, *done)
    query_grad, key_in, value_in, back, gain_grad = done

    gain_grad = gain_grad.transpose(2, 1, 0).reshape(seg_len, LEVELS * H)
    key_grad, value_grad = call(
        functools.partial(final_body, 4, gates), 2 * head_flops, 8 * tok_bytes, 56,
        out_shape=(sds((seg_len, width), BF),) * 2,
        grid_spec=prefetch(
            num_scalar_prefetch=1, grid=(H // 4,),
            in_specs=[cols(4)] * 2 + [turned(4)] * 2 + [stack(n_blocks, 4)] + [mat(4)] * len(got)
            + [pl.BlockSpec(memory_space=pl.ANY)],
            out_specs=(cols(4), cols(4)),
        ),
    )(bits, k, v, key_in, value_in, back, *got, gain_grad)
    return query_grad, key_grad, value_grad, gain_grad, weight_grad


def reduce_weight(attn, dout, dout_pair, batch_index, seq_count):
    width, seg_len = attn.shape
    quarter = width // 4
    core = batch_index & 1
    attn_pair = swapped(attn, "batch", 1)
    half = core.astype(jnp.int32)[None]

    def products(picks, dtype):
        lhs = pl.BlockSpec((4 * HD, seg_len), lambda j, c: (j, 0))
        grads = [pl.BlockSpec((seg_len, quarter), lambda j, c, n=n: (0, 2 * c[0] + n)) for n in (0, 0, 1, 1)]
        out = pl.BlockSpec((2 * HD, quarter), lambda j, c: (j, 0))
        return call(
            functools.partial(weight_body, picks), 4 * seg_len * width * quarter,
            2 * seg_len * (width + 2 * quarter) * 2 + width * quarter * 2,
            out_shape=(sds((width // 2, quarter), dtype),) * 2,
            grid_spec=pltpu.PrefetchScalarGridSpec(
                num_scalar_prefetch=1, grid=(width // (4 * HD),),
                in_specs=[lhs, lhs] + grads, out_specs=(out, out),
            ),
        )(half, attn, attn_pair, dout, dout_pair, dout, dout_pair)

    send_x, send_y = products(((1, 3), (2, 3)), BF)
    got_x = swapped(send_x, "batch", 2)
    got_y = swapped(send_y, "batch", 4)
    keep_x, keep_y = products(((0, 2), (0, 1)), F32)

    def pick(array, which):
        return array.reshape(seq_count, 2, HD, quarter)[:, which].astype(F32)

    send_xy = (pick(keep_x, 1) + pick(got_x, 1)).astype(BF)
    send_yx = (pick(keep_y, 1) + pick(got_y, 1)).astype(BF)
    got_xy = swapped(send_xy, "batch", 4)
    got_yx = swapped(send_yx, "batch", 2)
    left = pick(keep_x, 0) + pick(got_x, 0) + got_xy.astype(F32)
    right = pick(keep_y, 0) + pick(got_y, 0) + got_yx.astype(F32)
    total = jnp.concatenate([left, right], axis=2).reshape(2, 2, HD, width // 2)
    got_z = swapped(total[:, 1].astype(BF), "seq", 1)
    got_zz = swapped((total[1, 0] + got_z[1].astype(F32)).astype(BF), "seq", 2)
    mine = total[0, 0] + got_z[0].astype(F32) + got_zz.astype(F32)
    rows = mine.shape[0] // 2
    other = swapped(lax.dynamic_slice_in_dim(mine, (1 - core) * rows, rows, 0), "batch", 1)
    own = lax.dynamic_slice_in_dim(mine, core * rows, rows, 0)
    return jnp.where(
        core == 0, jnp.concatenate([own, other], axis=1), jnp.concatenate([other, own], axis=1)
    )


def solution(mesh):
    row = P("batch", "seq", None)
    return jax.shard_map(
        local,
        mesh=mesh,
        in_specs=(row, row, row, row, P("batch", None), row),
        out_specs=(row, row, row, row, P(("seq", "batch"), None)),
        check_vma=False,
    )
```
